256 devices in a mesh: kv: 4 (over y), seq: 64 (over z, x, core).
Axes of the slice: x: 4, y: 4, z: 8, core: 2. Of those that a mesh axis runs over, the one named last changes fastest.
Arguments:
- queries: bfloat16 [4096, 4, 8192], P('seq', 'kv'), may hold values from -41 to 41
- key_state_rows: bfloat16 [4096, 4, 1024], P('seq', 'kv'), may hold values from -6 to 6
- value_state_rows: bfloat16 [4096, 4, 1024], P('seq', 'kv'), may hold values from -6 to 6
- output_gradient: bfloat16 [16384, 8192], P('seq', 'kv'), may hold values from -6 to 6
- parents: int32 [128], replicated, may hold values from -1 to 126, as said below
Outputs:
- attended: bfloat16 [16384, 8192], P('seq', 'kv')
- query_grad: bfloat16 [4096, 4, 8192], P('seq', 'kv')
- key_gradient_rows: bfloat16 [4096, 4, 1024], P('seq', 'kv')
- value_gradient_rows: bfloat16 [4096, 4, 1024], P('seq', 'kv')
The draws below stay inside these ranges and needn't reach their ends.
Inputs may be any that keep to these rules, and one draw needn't show every extreme that they name: parents[b] is -1 for a tree's root and otherwise a block of the same tree below b. The blocks of a tree are consecutive, a tree begins at the first block of a device and covers at most 5 consecutive devices, so every ancestor of block b lies at block 2 * (b // 2 - 4) or above; in every draw some tree covers 4 + 1 devices.
All inputs are finite; a program needn't handle non-finite values.
Results may differ from the reference program's by a relative error of at most 0.034.
Values may be sent and summed in bfloat16 or wider, within the bound.
No kernel may reach another device: no remote copies, remote signals or barrier semaphores. Data moves between devices by JAX's collectives and lax.ppermute only.
A program may use at most 64 MiB of HBM per device.

```python
import math
import jax
import jax.numpy as jnp
from jax import lax

QUERY_HEADS = 64
KEY_VALUE_HEADS = 8
HEAD_WIDTH = 128
BLK = 128
REACH = 4
BLK_DEV = 2
TREE_TOKENS = 16384
BLOCKS = 128
N_KV = 4


def drawn_pair(key):
    base_key = jax.random.fold_in(key, 7)
    query_random_key, state_random_key = jax.random.split(base_key, 2)
    heads_per_group = QUERY_HEADS // KEY_VALUE_HEADS
    state_rows = jnp.clip(jax.random.normal(state_random_key, (TREE_TOKENS, KEY_VALUE_HEADS, HEAD_WIDTH), jnp.float32), -6.0, 6.0)
    queries = jnp.clip(jax.random.normal(query_random_key, (TREE_TOKENS, KEY_VALUE_HEADS, heads_per_group, HEAD_WIDTH), jnp.float32), -6.0, 6.0)
    return (queries, state_rows)


def draw_queries(key, part):
    queries, state_rows = drawn_pair(key)
    return queries.reshape(TREE_TOKENS // N_KV, N_KV, QUERY_HEADS * HEAD_WIDTH).astype(jnp.bfloat16)


def draw_key_state_rows(key, part):
    queries, state_rows = drawn_pair(key)
    return state_rows.reshape(TREE_TOKENS // N_KV, N_KV, KEY_VALUE_HEADS * HEAD_WIDTH).astype(jnp.bfloat16)


def draw_parents(key, part):
    base_key = jax.random.fold_in(key, 11)
    span_key, follow_key, offset_key = jax.random.split(base_key, 3)
    device_count = BLOCKS // BLK_DEV
    tree_span = jax.random.randint(span_key, (device_count,), 1, REACH + 2)
    tree_span = tree_span.at[0].set(REACH + 1)
    tree_first = jnp.cumsum(tree_span) - tree_span
    device_ids = jnp.arange(device_count, dtype=jnp.int32)
    starts = jnp.any(tree_first[:, None] == device_ids[None, :], axis=0)
    tree_start = lax.cummax(jnp.where(starts, device_ids, 0), axis=0)
    block_ids = jnp.arange(BLOCKS, dtype=jnp.int32)
    lowest = tree_start[block_ids // BLK_DEV] * BLK_DEV
    follow = jax.random.randint(follow_key, (BLOCKS,), 0, 2) == 0
    offset = jax.random.randint(offset_key, (BLOCKS,), 0, jnp.maximum(block_ids - lowest, 1))
    chosen_parent = jnp.where(follow, block_ids - 1, lowest + offset)
    return jnp.where(block_ids == lowest, -1, chosen_parent).astype(jnp.int32)


def steps_of(key, shape, cuts, smallest, high):
    factor_of = 1.0
    for dim, shards_of in cuts:
        draws = jax.random.uniform(jax.random.fold_in(jax.random.fold_in(key, 6), dim), (shards_of,), jnp.float32, smallest / len(cuts), high / len(cuts))
        factor_of = factor_of * jnp.repeat(jnp.exp(draws), shape[dim] // shards_of).reshape((-1,) + (1,) * (len(shape) - 1 - dim))
    return factor_of


def bell_draw(key, extent, width, bound, shards=(), kind=jnp.bfloat16):
    entries = jax.random.normal(key, extent, jnp.float32) * width
    if len(shards) > 0:
        entries = steps_of(key, extent, shards, -0.22, 0.18) * entries
    return jnp.clip(entries, min=-bound, max=bound).astype(kind)


def setup_inputs(seed: int = 0) -> dict:
    key_list = jax.random.split(jax.random.key(seed), 6)
    queries = draw_queries(jax.random.fold_in(key_list[5], 71), 0)
    key_state_rows = draw_key_state_rows(jax.random.fold_in(key_list[5], 71), 0)
    value_state_rows = bell_draw(key_list[2], (TREE_TOKENS // N_KV, N_KV, KEY_VALUE_HEADS * HEAD_WIDTH), 1.0, 6.0, ((0, 64), (1, 4)))
    output_gradient = bell_draw(key_list[3], (TREE_TOKENS, QUERY_HEADS * HEAD_WIDTH), 1.0, 6.0, ((0, 64), (1, 4)))
    parents = draw_parents(jax.random.fold_in(key_list[5], 71), 0)
    return {"queries": queries, "key_state_rows": key_state_rows, "value_state_rows": value_state_rows, "output_gradient": output_gradient, "parents": parents}


LOW_LOGIT = -1e+30

def ancestor_table(parents):
    block_ids = jnp.arange(BLOCKS, dtype=jnp.int32)
    table = jnp.zeros((BLOCKS, BLOCKS), dtype=bool)
    current = parents.astype(jnp.int32)
    for level in range(BLK_DEV * (REACH + 1)):
        table = table | (current[:, None] == block_ids[None, :]) & (current[:, None] >= 0)
        current = jnp.where(current >= 0, parents[jnp.maximum(current, 0)], -1).astype(jnp.int32)
    return table

def reference(queries, key_state_rows, value_state_rows, output_gradient, parents):
    heads_per_group = QUERY_HEADS // KEY_VALUE_HEADS
    inverse_root = 1.0 / math.sqrt(HEAD_WIDTH)
    window_tokens = BLK_DEV * (REACH + 1) * BLK
    query_everything = queries.reshape(TREE_TOKENS, KEY_VALUE_HEADS, heads_per_group, HEAD_WIDTH)
    key_everything = key_state_rows.reshape(TREE_TOKENS, KEY_VALUE_HEADS, HEAD_WIDTH)
    value_everything = value_state_rows.reshape(TREE_TOKENS, KEY_VALUE_HEADS, HEAD_WIDTH)
    gradient_everything = output_gradient.reshape(TREE_TOKENS, KEY_VALUE_HEADS, heads_per_group, HEAD_WIDTH)
    table = ancestor_table(parents)
    query_position = jnp.arange(BLK, dtype=jnp.int32)

    def one_block(running, q_block):
        key_gradients, value_gradients = running
        device = q_block // BLK_DEV
        start_blk = (jnp.maximum(device - REACH, 0) * BLK_DEV).astype(jnp.int32)
        start = (start_blk * BLK).astype(jnp.int32)
        row_start = (q_block * BLK).astype(jnp.int32)
        q_tile = lax.dynamic_slice_in_dim(query_everything, row_start, BLK, 0).astype(jnp.float32)
        g_tile = lax.dynamic_slice_in_dim(gradient_everything, row_start, BLK, 0).astype(jnp.float32)
        key_window = lax.dynamic_slice_in_dim(key_everything, start, window_tokens, 0).astype(jnp.float32)
        value_window = lax.dynamic_slice_in_dim(value_everything, start, window_tokens, 0).astype(jnp.float32)
        key_block = start_blk + jnp.arange(window_tokens, dtype=jnp.int32) // BLK
        key_position = jnp.arange(window_tokens, dtype=jnp.int32) % BLK
        linked = table[q_block][key_block]
        same_block = key_block == q_block
        allowed = linked[None, :] | same_block[None, :] & (key_position[None, :] <= query_position[:, None])
        logits = jnp.einsum('ihgd,jhd->hgij', q_tile, key_window) * inverse_root
        row_peak = lax.optimization_barrier(jnp.max(jnp.where(allowed, logits, LOW_LOGIT), axis=-1))
        expsum = lax.optimization_barrier(jnp.sum(jnp.where(allowed, jnp.exp(logits - row_peak[..., None]), 0.0), axis=-1))
        log_total = row_peak + jnp.log(expsum)
        exact_probs = jnp.where(allowed, jnp.exp(logits - log_total[..., None]), 0.0)
        rounded_probs = lax.optimization_barrier(exact_probs.astype(jnp.bfloat16)).astype(jnp.float32)
        attended = jnp.einsum('hgij,jhd->ihgd', rounded_probs, value_window).astype(jnp.bfloat16)
        row_dot = jnp.einsum('ihgd,ihgd->hgi', g_tile, attended.astype(jnp.float32))
        dprobs = jnp.einsum('ihgd,jhd->hgij', g_tile, value_window)
        dlogits = exact_probs * (dprobs - row_dot[..., None]) * inverse_root
        dlogits = lax.optimization_barrier(dlogits.astype(jnp.bfloat16)).astype(jnp.float32)
        query_part = jnp.einsum('hgij,jhd->ihgd', dlogits, key_window).astype(jnp.bfloat16)
        key_part = jnp.einsum('hgij,ihgd->jhd', dlogits, q_tile)
        value_part = jnp.einsum('hgij,ihgd->jhd', rounded_probs, g_tile)
        old_keys = lax.dynamic_slice_in_dim(key_gradients, start, window_tokens, 0)
        key_gradients = lax.dynamic_update_slice_in_dim(key_gradients, old_keys + key_part, start, 0)
        old_values = lax.dynamic_slice_in_dim(value_gradients, start, window_tokens, 0)
        value_gradients = lax.dynamic_update_slice_in_dim(value_gradients, old_values + value_part, start, 0)
        return ((key_gradients, value_gradients), (attended, query_part))
    zero_key_values = jnp.zeros((TREE_TOKENS, KEY_VALUE_HEADS, HEAD_WIDTH), jnp.float32)
    (key_gradients, value_gradients), (attended, query_part) = lax.scan(one_block, (zero_key_values, zero_key_values), jnp.arange(BLOCKS, dtype=jnp.int32))
    attended = attended.reshape(TREE_TOKENS, QUERY_HEADS * HEAD_WIDTH)
    query_grad = query_part.reshape(TREE_TOKENS // N_KV, N_KV, QUERY_HEADS * HEAD_WIDTH)
    key_gradient_rows = key_gradients.astype(jnp.bfloat16).reshape(TREE_TOKENS // N_KV, N_KV, KEY_VALUE_HEADS * HEAD_WIDTH)
    value_gradient_rows = value_gradients.astype(jnp.bfloat16).reshape(TREE_TOKENS // N_KV, N_KV, KEY_VALUE_HEADS * HEAD_WIDTH)
    return (attended, query_grad, key_gradient_rows, value_gradient_rows)
```

```python
import functools
import math

import jax
import jax.numpy as jnp
from jax import lax
from jax.experimental import pallas as pl
from jax.experimental.pallas import tpu as pltpu
from jax.sharding import Mesh
from jax.sharding import PartitionSpec as P

QUERY_HEADS = 64
KEY_VALUE_HEADS = 8
HEADS_PER_GROUP = QUERY_HEADS // KEY_VALUE_HEADS
D = 128
BLK = 128
N_KV = 4
CORES = 2
REACH_CHIPS = 2
CHIP_BLOCKS = 4
WINDOW = CHIP_BLOCKS * (REACH_CHIPS + 1)
MAX_PAIRS = 5
QUARTER = BLK // N_KV
ROWS = HEADS_PER_GROUP * BLK
GROUP = HEADS_PER_GROUP * D
LOW_LOGIT = -1e30
INVERSE_ROOT = 1.0 / math.sqrt(D)
EXP2_FACTOR = INVERSE_ROOT / math.log(2.0)
F32 = jnp.float32
BF16 = jnp.bfloat16

NN = (((1,), (0,)), ((), ()))
NT = (((1,), (1,)), ((), ()))
TN = (((0,), (0,)), ((), ()))


def dot(a, b, dims=NN):
    return lax.dot_general(a, b, dims, preferred_element_type=F32)


def position(index):
    return N_KV * (index % QUARTER) + index // QUARTER


def attention_kernel(
    place_ref,
    parents_ref,
    q_ref,
    g_own_ref,
    g_other_ref,
    kv_here_ref,
    kv_one_ref,
    kv_two_ref,
    att_own_ref,
    att_other_ref,
    dq_ref,
    d_here_ref,
    d_one_ref,
    d_two_ref,
    tiles,
    keys,
    values,
    queries,
    grads,
    logits,
    peaks,
    attended,
    query_grad,
    weights,
    dlogits,
    key_grad,
    value_grad,
):
    chip = place_ref[0]
    core = place_ref[1]
    base = (chip - REACH_CHIPS) * CHIP_BLOCKS

    for source, ref in enumerate((kv_two_ref, kv_one_ref, kv_here_ref)):
        for block in range(CHIP_BLOCKS):
            window = source * CHIP_BLOCKS + block
            rows = slice((block % 2) * QUARTER, (block % 2 + 1) * QUARTER)
            for k in range(N_KV):
                out = slice(k * QUARTER, (k + 1) * QUARTER)
                keys[window, out, :] = ref[k, block // 2, rows, 0:D]
                values[window, out, :] = ref[k, block // 2, rows, D : 2 * D]
    key_grad[...] = jnp.zeros_like(key_grad)
    value_grad[...] = jnp.zeros_like(value_grad)

    row_i = lax.broadcasted_iota(jnp.int32, (BLK, BLK), 0)
    col_i = lax.broadcasted_iota(jnp.int32, (BLK, BLK), 1)
    to_slots = (position(row_i) == col_i).astype(BF16)
    to_tokens = (row_i == position(col_i)).astype(BF16)
    causal = position(row_i) >= position(col_i)

    def one_block(step, unused):
        slot = step // 2
        half = step % 2
        owner = jnp.where(slot == 0, core, 1 - core)
        own_window = REACH_CHIPS * CHIP_BLOCKS + owner * 2 + half
        quarter = pl.multiple_of(half * QUARTER, QUARTER)
        half_rows = pl.ds(pl.multiple_of(half * BLK, BLK), BLK)

        tiles[0] = own_window

        def climb(unused, running):
            current, count = running
            found = current >= 0

            @pl.when(found)
            def _():
                tiles[count + 2] = current - base

            following = parents_ref[jnp.maximum(current, 0)]
            return (
                jnp.where(found, following, -1),
                jnp.where(found, count + 1, count),
            )

        start = parents_ref[base + own_window]
        _, count = lax.fori_loop(0, 2 * MAX_PAIRS - 1, climb, (start, jnp.int32(0)))
        odd = count % 2 == 1
        tiles[1] = jnp.where(odd, tiles[jnp.where(odd, count + 1, 0)], own_window)
        pairs = count // 2 + 1

        for h in range(HEADS_PER_GROUP):
            for k in range(N_KV):
                queries[h * BLK + k * QUARTER : h * BLK + (k + 1) * QUARTER, :] = q_ref[
                    k, owner, pl.ds(quarter, QUARTER), h * D : (h + 1) * D
                ]

        def load_grads(ref):
            slots = dot(to_slots, ref[half_rows, :]).astype(BF16)
            for h in range(HEADS_PER_GROUP):
                grads[h * BLK : (h + 1) * BLK, :] = slots[:, h * D : (h + 1) * D]

        pl.when(slot == 0)(lambda: load_grads(g_own_ref))
        pl.when(slot == 1)(lambda: load_grads(g_other_ref))

        def pair_of(ref, pair):
            return jnp.concatenate([ref[tiles[2 * pair]], ref[tiles[2 * pair + 1]]], axis=0)

        first = dot(queries[...], pair_of(keys, 0), NT)
        for h in range(HEADS_PER_GROUP):
            rows = slice(h * BLK, (h + 1) * BLK)
            left = jnp.where(causal, first[rows, :BLK], LOW_LOGIT)
            right = jnp.where(odd, first[rows, BLK:], LOW_LOGIT)
            logits[0, rows, :BLK] = left
            logits[0, rows, BLK:] = right
            peaks[rows, :] = jnp.maximum(left, right)

        def logit_step(pair, unused):
            scores = dot(queries[...], pair_of(keys, pair), NT)
            logits[pair] = scores
            peaks[...] = jnp.maximum(
                peaks[...], jnp.maximum(scores[:, :BLK], scores[:, BLK:])
            )
            return unused

        lax.fori_loop(1, pairs, logit_step, 0)
        peak = jnp.max(peaks[...], axis=1, keepdims=True) * EXP2_FACTOR
        peaks[...] = jnp.broadcast_to(peak, (ROWS, BLK))
        attended[...] = jnp.zeros_like(attended)
        query_grad[...] = jnp.zeros_like(query_grad)

        def out_step(pair, unused):
            for h in range(HEADS_PER_GROUP):
                rows = slice(h * BLK, (h + 1) * BLK)
                peak = peaks[rows, :]
                left = jnp.exp2(logits[pair, rows, :BLK] * EXP2_FACTOR - peak)
                right = jnp.exp2(logits[pair, rows, BLK:] * EXP2_FACTOR - peak)
                logits[pair, rows, :BLK] = left
                logits[pair, rows, BLK:] = right
                weights[rows, :BLK] = left.astype(BF16)
                weights[rows, BLK:] = right.astype(BF16)
                query_grad[rows, :] += left + right
            attended[...] += dot(weights[...], pair_of(values, pair))
            return unused

        lax.fori_loop(0, pairs, out_step, 0)
        total = jnp.sum(query_grad[...], axis=1, keepdims=True)
        inverse = 1.0 / total
        rounded = (attended[...] * inverse).astype(BF16)
        row_dot = jnp.sum(
            grads[...].astype(F32) * rounded.astype(F32), axis=1, keepdims=True
        )
        peaks[...] = jnp.broadcast_to(inverse, (ROWS, BLK))
        attended[...] = jnp.broadcast_to(row_dot, (ROWS, BLK))
        wide = jnp.concatenate(
            [rounded[h * BLK : (h + 1) * BLK] for h in range(HEADS_PER_GROUP)], axis=1
        )
        in_tokens = dot(to_tokens, wide).astype(BF16)

        @pl.when(slot == 0)
        def _():
            att_own_ref[half_rows, :] = in_tokens

        @pl.when(slot == 1)
        def _():
            att_other_ref[half_rows, :] = in_tokens

        query_grad[...] = jnp.zeros_like(query_grad)

        def back_step(pair, unused):
            dprobs = dot(grads[...], pair_of(values, pair), NT)
            for h in range(HEADS_PER_GROUP):
                rows = slice(h * BLK, (h + 1) * BLK)
                for part in range(2):
                    cols = slice(part * BLK, (part + 1) * BLK)
                    probs = logits[pair, rows, cols] * peaks[rows, :]
                    weights[rows, cols] = probs.astype(BF16)
                    dlogits[rows, cols] = (
                        probs * (dprobs[rows, cols] - attended[rows, :])
                    ).astype(BF16)
            query_grad[...] += dot(dlogits[...], pair_of(keys, pair))
            key_part = dot(dlogits[...], queries[...], TN)
            value_part = dot(weights[...], grads[...], TN)
            for part in range(2):
                rows = slice(part * BLK, (part + 1) * BLK)
                window = tiles[2 * pair + part]
                key_grad[window] += key_part[rows, :]
                value_grad[window] += value_part[rows, :]
            return unused

        lax.fori_loop(0, pairs, back_step, 0)
        for h in range(HEADS_PER_GROUP):
            for k in range(N_KV):
                rows = slice(h * BLK + k * QUARTER, h * BLK + (k + 1) * QUARTER)
                dq_ref[k, owner, pl.ds(quarter, QUARTER), h * D : (h + 1) * D] = (
                    query_grad[rows, :] * INVERSE_ROOT
                ).astype(BF16)
        return unused

    lax.fori_loop(0, CHIP_BLOCKS, one_block, 0)

    for source, ref in enumerate((d_two_ref, d_one_ref, d_here_ref)):
        for block in range(CHIP_BLOCKS):
            window = source * CHIP_BLOCKS + block
            rows = slice((block % 2) * QUARTER, (block % 2 + 1) * QUARTER)
            for k in range(N_KV):
                part = slice(k * QUARTER, (k + 1) * QUARTER)
                ref[k, block // 2, rows, 0:D] = (
                    key_grad[window, part, :] * INVERSE_ROOT
                ).astype(ref.dtype)
                ref[k, block // 2, rows, D : 2 * D] = value_grad[window, part, :].astype(
                    ref.dtype
                )


def attention(place, parents, q, g_own, g_other, kv_here, kv_one, kv_two):
    vmem = pl.BlockSpec(memory_space=pltpu.VMEM)
    smem = pl.BlockSpec(memory_space=pltpu.SMEM)
    return pl.pallas_call(
        attention_kernel,
        out_shape=(
            jax.ShapeDtypeStruct(g_own.shape, BF16),
            jax.ShapeDtypeStruct(g_other.shape, BF16),
            jax.ShapeDtypeStruct(q.shape, BF16),
            jax.ShapeDtypeStruct(kv_here.shape, F32),
            jax.ShapeDtypeStruct(kv_one.shape, BF16),
            jax.ShapeDtypeStruct(kv_two.shape, BF16),
        ),
        in_specs=[smem, smem] + [vmem] * 6,
        out_specs=(vmem,) * 6,
        scratch_shapes=[
            pltpu.SMEM((2 * MAX_PAIRS + 2,), jnp.int32),
            pltpu.VMEM((WINDOW, BLK, D), BF16),
            pltpu.VMEM((WINDOW, BLK, D), BF16),
            pltpu.VMEM((ROWS, D), BF16),
            pltpu.VMEM((ROWS, D), BF16),
            pltpu.VMEM((MAX_PAIRS, ROWS, 2 * BLK), F32),
            pltpu.VMEM((ROWS, BLK), F32),
            pltpu.VMEM((ROWS, D), F32),
            pltpu.VMEM((ROWS, D), F32),
            pltpu.VMEM((ROWS, 2 * BLK), BF16),
            pltpu.VMEM((ROWS, 2 * BLK), BF16),
            pltpu.VMEM((WINDOW, BLK, D), F32),
            pltpu.VMEM((WINDOW, BLK, D), F32),
        ],
        compiler_params=pltpu.CompilerParams(vmem_limit_bytes=48 << 20),
        name="tree_attention",
    )(place, parents, q, g_own, g_other, kv_here, kv_one, kv_two)


def along_chips(value, by):
    chips = lax.axis_size("chip")
    return lax.ppermute(value, "chip", [(i, (i + by) % chips) for i in range(chips)])


def core_swap(value):
    return lax.ppermute(value, "core", [(0, 1), (1, 0)])


def exchange(value):
    return lax.all_to_all(value, ("kv", "core"), split_axis=0, concat_axis=0, tiled=True)


def local(queries, key_state_rows, value_state_rows, output_gradient, parents):
    rows = queries.shape[0]
    core = lax.axis_index("core")
    chip = lax.axis_index("chip")
    groups = KEY_VALUE_HEADS

    def split_groups(value, width):
        return value.reshape(rows, groups, width)

    kv_send = jnp.concatenate(
        [split_groups(key_state_rows, D), split_groups(value_state_rows, D)], axis=2
    ).transpose(1, 0, 2)
    kv_here = exchange(kv_send).reshape(N_KV, CORES, rows, 2 * D)
    g_own = lax.dynamic_slice_in_dim(output_gradient, core * GROUP, GROUP, axis=1)
    g_other = core_swap(
        lax.dynamic_slice_in_dim(output_gradient, (1 - core) * GROUP, GROUP, axis=1)
    )
    kv_one = along_chips(kv_here, 1)
    kv_two = along_chips(kv_here, 2)
    q = exchange(split_groups(queries, GROUP).transpose(1, 0, 2)).reshape(
        N_KV, CORES, rows, GROUP
    )
    place = jnp.stack([chip, core]).astype(jnp.int32)
    att_own, att_other, dq, d_here, d_one, d_two = attention(
        place, parents, q, g_own, g_other, kv_here, kv_one, kv_two
    )
    att_received = core_swap(att_other)
    attended = jnp.where(
        core == 0,
        jnp.concatenate([att_own, att_received], axis=1),
        jnp.concatenate([att_received, att_own], axis=1),
    )
    summed = (
        d_here
        + along_chips(d_one, -1).astype(F32)
        + along_chips(d_two, -2).astype(F32)
    ).astype(BF16)
    d_kv = exchange(summed.reshape(groups, rows, 2 * D)).transpose(1, 0, 2)
    d_q = exchange(dq.reshape(groups, rows, GROUP)).transpose(1, 0, 2)
    return (
        attended,
        d_q.reshape(rows, 1, QUERY_HEADS * D),
        d_kv[:, :, :D].reshape(rows, 1, groups * D),
        d_kv[:, :, D:].reshape(rows, 1, groups * D),
    )


def solution(mesh):
    fine = Mesh(
        mesh.devices.reshape(mesh.shape["kv"], mesh.shape["seq"] // CORES, CORES),
        ("kv", "chip", "core"),
    )
    tokens = P(("chip", "core"), "kv", None)
    flat = P(("chip", "core"), "kv")
    return jax.shard_map(
        local,
        mesh=fine,
        in_specs=(tokens, tokens, tokens, flat, P()),
        out_specs=(flat, tokens, tokens, tokens),
        check_vma=False,
    )
```

```python
import functools
import math

import jax
import jax.numpy as jnp
from jax import lax
from jax.experimental import pallas as pl
from jax.experimental.pallas import tpu as pltpu
from jax.sharding import Mesh
from jax.sharding import PartitionSpec as P

QUERY_HEADS = 64
KEY_VALUE_HEADS = 8
HEADS_PER_GROUP = QUERY_HEADS // KEY_VALUE_HEADS
D = 128
BLK = 128
N_KV = 4
CORES = 2
REACH_CHIPS = 2
CHIP_BLOCKS = 4
WINDOW = CHIP_BLOCKS * (REACH_CHIPS + 1)
MAX_PAIRS = 5
QUARTER = BLK // N_KV
ROWS = HEADS_PER_GROUP * BLK
GROUP = HEADS_PER_GROUP * D
LOW_LOGIT = -1e30
INVERSE_ROOT = 1.0 / math.sqrt(D)
EXP2_FACTOR = INVERSE_ROOT / math.log(2.0)
F32 = jnp.float32
BF16 = jnp.bfloat16

NN = (((1,), (0,)), ((), ()))
NT = (((1,), (1,)), ((), ()))
TN = (((0,), (0,)), ((), ()))


def dot(a, b, dims=NN):
    return lax.dot_general(a, b, dims, preferred_element_type=F32)


def position(index):
    return N_KV * (index % QUARTER) + index // QUARTER


def attention_kernel(
    place_ref,
    parents_ref,
    q_ref,
    g_own_ref,
    g_other_ref,
    kv_here_ref,
    kv_one_ref,
    kv_two_ref,
    att_own_ref,
    att_other_ref,
    dq_ref,
    d_here_ref,
    d_one_ref,
    d_two_ref,
    tiles,
    keys,
    values,
    queries,
    grads,
    logits,
    peaks,
    attended,
    query_grad,
    weights,
    dlogits,
    key_grad,
    value_grad,
):
    chip = place_ref[0]
    core = place_ref[1]
    base = (chip - REACH_CHIPS) * CHIP_BLOCKS

    for source, ref in enumerate((kv_two_ref, kv_one_ref, kv_here_ref)):
        for block in range(CHIP_BLOCKS):
            window = source * CHIP_BLOCKS + block
            rows = slice((block % 2) * QUARTER, (block % 2 + 1) * QUARTER)
            for k in range(N_KV):
                out = slice(k * QUARTER, (k + 1) * QUARTER)
                keys[window, out, :] = ref[k, block // 2, rows, 0:D]
                values[window, out, :] = ref[k, block // 2, rows, D : 2 * D]
    key_grad[...] = jnp.zeros_like(key_grad)
    value_grad[...] = jnp.zeros_like(value_grad)

    row_i = lax.broadcasted_iota(jnp.int32, (BLK, BLK), 0)
    col_i = lax.broadcasted_iota(jnp.int32, (BLK, BLK), 1)
    to_slots = (position(row_i) == col_i).astype(BF16)
    to_tokens = (row_i == position(col_i)).astype(BF16)
    causal = position(row_i) >= position(col_i)

    def one_block(step, unused):
        slot = step // 2
        half = step % 2
        owner = jnp.where(slot == 0, core, 1 - core)
        own_window = REACH_CHIPS * CHIP_BLOCKS + owner * 2 + half
        quarter = pl.multiple_of(half * QUARTER, QUARTER)
        half_rows = pl.ds(pl.multiple_of(half * BLK, BLK), BLK)

        tiles[0] = own_window

        def climb(unused, running):
            current, count = running
            found = current >= 0

            @pl.when(found)
            def _():
                tiles[count + 2] = current - base

            following = parents_ref[jnp.maximum(current, 0)]
            return (
                jnp.where(found, following, -1),
                jnp.where(found, count + 1, count),
            )

        start = parents_ref[base + own_window]
        _, count = lax.fori_loop(0, 2 * MAX_PAIRS - 1, climb, (start, jnp.int32(0)))
        odd = count % 2 == 1
        tiles[1] = jnp.where(odd, tiles[jnp.where(odd, count + 1, 0)], own_window)
        pairs = count // 2 + 1

        for h in range(HEADS_PER_GROUP):
            for k in range(N_KV):
                queries[h * BLK + k * QUARTER : h * BLK + (k + 1) * QUARTER, :] = q_ref[
                    k, owner, pl.ds(quarter, QUARTER), h * D : (h + 1) * D
                ]

        def load_grads(ref):
            slots = dot(to_slots, ref[half_rows, :]).astype(BF16)
            for h in range(HEADS_PER_GROUP):
                grads[h * BLK : (h + 1) * BLK, :] = slots[:, h * D : (h + 1) * D]

        pl.when(slot == 0)(lambda: load_grads(g_own_ref))
        pl.when(slot == 1)(lambda: load_grads(g_other_ref))

        def pair_of(ref, pair):
            return jnp.concatenate([ref[tiles[2 * pair]], ref[tiles[2 * pair + 1]]], axis=0)

        first = dot(queries[...], pair_of(keys, 0), NT)
        for h in range(HEADS_PER_GROUP):
            rows = slice(h * BLK, (h + 1) * BLK)
            left = jnp.where(causal, first[rows, :BLK], LOW_LOGIT)
            right = jnp.where(odd, first[rows, BLK:], LOW_LOGIT)
            logits[0, rows, :BLK] = left
            logits[0, rows, BLK:] = right
            peaks[rows, :] = jnp.maximum(left, right)

        def logit_step(pair, unused):
            scores = dot(queries[...], pair_of(keys, pair), NT)
            logits[pair] = scores
            peaks[...] = jnp.maximum(
                peaks[...], jnp.maximum(scores[:, :BLK], scores[:, BLK:])
            )
            return unused

        lax.fori_loop(1, pairs, logit_step, 0)
        peak = jnp.max(peaks[...], axis=1, keepdims=True) * EXP2_FACTOR
        peaks[...] = jnp.broadcast_to(peak, (ROWS, BLK))
        attended[...] = jnp.zeros_like(attended)
        query_grad[...] = jnp.zeros_like(query_grad)

        def out_step(pair, unused):
            for h in range(HEADS_PER_GROUP):
                rows = slice(h * BLK, (h + 1) * BLK)
                peak = peaks[rows, :]
                left = jnp.exp2(logits[pair, rows, :BLK] * EXP2_FACTOR - peak)
                right = jnp.exp2(logits[pair, rows, BLK:] * EXP2_FACTOR - peak)
                logits[pair, rows, :BLK] = left
                logits[pair, rows, BLK:] = right
                weights[rows, :BLK] = left.astype(BF16)
                weights[rows, BLK:] = right.astype(BF16)
                query_grad[rows, :] += left + right
            attended[...] += dot(weights[...], pair_of(values, pair))
            return unused

        lax.fori_loop(0, pairs, out_step, 0)
        total = jnp.sum(query_grad[...], axis=1, keepdims=True)
        inverse = 1.0 / total
        rounded = (attended[...] * inverse).astype(BF16)
        row_dot = jnp.sum(
            grads[...].astype(F32) * rounded.astype(F32), axis=1, keepdims=True
        )
        peaks[...] = jnp.broadcast_to(inverse, (ROWS, BLK))
        attended[...] = jnp.broadcast_to(row_dot, (ROWS, BLK))
        wide = jnp.concatenate(
            [rounded[h * BLK : (h + 1) * BLK] for h in range(HEADS_PER_GROUP)], axis=1
        )
        in_tokens = dot(to_tokens, wide).astype(BF16)

        @pl.when(slot == 0)
        def _():
            att_own_ref[half_rows, :] = in_tokens

        @pl.when(slot == 1)
        def _():
            att_other_ref[half_rows, :] = in_tokens

        query_grad[...] = jnp.zeros_like(query_grad)

        def back_step(pair, unused):
            dprobs = dot(grads[...], pair_of(values, pair), NT)
            for h in range(HEADS_PER_GROUP):
                rows = slice(h * BLK, (h + 1) * BLK)
                for part in range(2):
                    cols = slice(part * BLK, (part + 1) * BLK)
                    probs = logits[pair, rows, cols] * peaks[rows, :]
                    weights[rows, cols] = probs.astype(BF16)
                    dlogits[rows, cols] = (
                        probs * (dprobs[rows, cols] - attended[rows, :])
                    ).astype(BF16)
            query_grad[...] += dot(dlogits[...], pair_of(keys, pair))
            key_part = dot(dlogits[...], queries[...], TN)
            value_part = dot(weights[...], grads[...], TN)
            for part in range(2):
                rows = slice(part * BLK, (part + 1) * BLK)
                window = tiles[2 * pair + part]
                key_grad[window] += key_part[rows, :]
                value_grad[window] += value_part[rows, :]
            return unused

        lax.fori_loop(0, pairs, back_step, 0)
        for h in range(HEADS_PER_GROUP):
            for k in range(N_KV):
                rows = slice(h * BLK + k * QUARTER, h * BLK + (k + 1) * QUARTER)
                dq_ref[k, owner, pl.ds(quarter, QUARTER), h * D : (h + 1) * D] = (
                    query_grad[rows, :] * INVERSE_ROOT
                ).astype(BF16)
        return unused

    lax.fori_loop(0, CHIP_BLOCKS, one_block, 0)

    for source, ref in enumerate((d_two_ref, d_one_ref, d_here_ref)):
        for block in range(CHIP_BLOCKS):
            window = source * CHIP_BLOCKS + block
            rows = slice((block % 2) * QUARTER, (block % 2 + 1) * QUARTER)
            for k in range(N_KV):
                part = slice(k * QUARTER, (k + 1) * QUARTER)
                ref[k, block // 2, rows, 0:D] = (
                    key_grad[window, part, :] * INVERSE_ROOT
                ).astype(ref.dtype)
                ref[k, block // 2, rows, D : 2 * D] = value_grad[window, part, :].astype(
                    ref.dtype
                )


def attention(place, parents, q, g_own, g_other, kv_here, kv_one, kv_two):
    vmem = pl.BlockSpec(memory_space=pltpu.VMEM)
    smem = pl.BlockSpec(memory_space=pltpu.SMEM)
    return pl.pallas_call(
        attention_kernel,
        out_shape=(
            jax.ShapeDtypeStruct(g_own.shape, BF16),
            jax.ShapeDtypeStruct(g_other.shape, BF16),
            jax.ShapeDtypeStruct(q.shape, BF16),
            jax.ShapeDtypeStruct(kv_here.shape, F32),
            jax.ShapeDtypeStruct(kv_one.shape, BF16),
            jax.ShapeDtypeStruct(kv_two.shape, BF16),
        ),
        in_specs=[smem, smem] + [vmem] * 6,
        out_specs=(vmem,) * 6,
        scratch_shapes=[
            pltpu.SMEM((2 * MAX_PAIRS + 2,), jnp.int32),
            pltpu.VMEM((WINDOW, BLK, D), BF16),
            pltpu.VMEM((WINDOW, BLK, D), BF16),
            pltpu.VMEM((ROWS, D), BF16),
            pltpu.VMEM((ROWS, D), BF16),
            pltpu.VMEM((MAX_PAIRS, ROWS, 2 * BLK), F32),
            pltpu.VMEM((ROWS, BLK), F32),
            pltpu.VMEM((ROWS, D), F32),
            pltpu.VMEM((ROWS, D), F32),
            pltpu.VMEM((ROWS, 2 * BLK), BF16),
            pltpu.VMEM((ROWS, 2 * BLK), BF16),
            pltpu.VMEM((WINDOW, BLK, D), F32),
            pltpu.VMEM((WINDOW, BLK, D), F32),
        ],
        compiler_params=pltpu.CompilerParams(vmem_limit_bytes=48 << 20),
        name="tree_attention",
    )(place, parents, q, g_own, g_other, kv_here, kv_one, kv_two)


def pack_kernel(k_ref, v_ref, out_ref):
    for h in range(KEY_VALUE_HEADS):
        cols = slice(h * D, (h + 1) * D)
        out_ref[h, :, 0:D] = k_ref[:, cols]
        out_ref[h, :, D : 2 * D] = v_ref[:, cols]


def pack(k, v):
    rows = k.shape[0]
    return pl.pallas_call(
        pack_kernel,
        out_shape=jax.ShapeDtypeStruct((KEY_VALUE_HEADS, rows, 2 * D), k.dtype),
        name="pack_keys_values",
    )(k, v)


def unpack_kernel(in_ref, k_ref, v_ref):
    for h in range(KEY_VALUE_HEADS):
        cols = slice(h * D, (h + 1) * D)
        k_ref[:, cols] = in_ref[h, :, 0:D]
        v_ref[:, cols] = in_ref[h, :, D : 2 * D]


def unpack(value):
    rows = value.shape[1]
    flat = jax.ShapeDtypeStruct((rows, KEY_VALUE_HEADS * D), value.dtype)
    return pl.pallas_call(
        unpack_kernel, out_shape=(flat, flat), name="unpack_keys_values"
    )(value)


def along_chips(value, by):
    chips = lax.axis_size("chip")
    return lax.ppermute(value, "chip", [(i, (i + by) % chips) for i in range(chips)])


def core_swap(value):
    return lax.ppermute(value, "core", [(0, 1), (1, 0)])


def exchange(value):
    return lax.all_to_all(value, ("kv", "core"), split_axis=0, concat_axis=0, tiled=True)


def local(queries, key_state_rows, value_state_rows, output_gradient, parents):
    rows = queries.shape[0]
    core = lax.axis_index("core")
    chip = lax.axis_index("chip")
    groups = KEY_VALUE_HEADS

    kv_here = exchange(
        pack(
            key_state_rows.reshape(rows, groups * D),
            value_state_rows.reshape(rows, groups * D),
        )
    )
    q_send = queries.reshape(rows, groups, GROUP).transpose(1, 0, 2)
    g_own = lax.dynamic_slice_in_dim(output_gradient, core * GROUP, GROUP, axis=1)
    g_send = lax.dynamic_slice_in_dim(
        output_gradient, (1 - core) * GROUP, GROUP, axis=1
    )
    kv_here, q_send, g_own, g_send = lax.optimization_barrier(
        (kv_here, q_send, g_own, g_send)
    )
    kv_here = kv_here.reshape(N_KV, CORES, rows, 2 * D)
    g_other = core_swap(g_send)
    kv_one = along_chips(kv_here, 1)
    kv_two = along_chips(kv_here, 2)
    q = exchange(q_send).reshape(N_KV, CORES, rows, GROUP)
    place = jnp.stack([chip, core]).astype(jnp.int32)
    att_own, att_other, dq, d_here, d_one, d_two = attention(
        place, parents, q, g_own, g_other, kv_here, kv_one, kv_two
    )
    att_received = core_swap(att_other)
    attended = jnp.where(
        core == 0,
        jnp.concatenate([att_own, att_received], axis=1),
        jnp.concatenate([att_received, att_own], axis=1),
    )
    summed = (
        d_here
        + along_chips(d_one, -1).astype(F32)
        + along_chips(d_two, -2).astype(F32)
    ).astype(BF16)
    d_q, summed = lax.optimization_barrier(
        (exchange(dq.reshape(groups, rows, GROUP)), summed)
    )
    d_k, d_v = unpack(exchange(summed.reshape(groups, rows, 2 * D)))
    return (
        attended,
        d_q.transpose(1, 0, 2).reshape(rows, 1, QUERY_HEADS * D),
        d_k.reshape(rows, 1, groups * D),
        d_v.reshape(rows, 1, groups * D),
    )


def solution(mesh):
    fine = Mesh(
        mesh.devices.reshape(mesh.shape["kv"], mesh.shape["seq"] // CORES, CORES),
        ("kv", "chip", "core"),
    )
    tokens = P(("chip", "core"), "kv", None)
    flat = P(("chip", "core"), "kv")
    return jax.shard_map(
        local,
        mesh=fine,
        in_specs=(tokens, tokens, tokens, flat, P()),
        out_specs=(flat, tokens, tokens, tokens),
        check_vma=False,
    )
```

```python
import functools
import math

import jax
import jax.numpy as jnp
from jax import lax
from jax.experimental import pallas as pl
from jax.experimental.pallas import tpu as pltpu
from jax.sharding import Mesh
from jax.sharding import PartitionSpec as P

QUERY_HEADS = 64
KEY_VALUE_HEADS = 8
HEADS_PER_GROUP = QUERY_HEADS // KEY_VALUE_HEADS
D = 128
BLK = 128
N_KV = 4
CORES = 2
REACH_CHIPS = 2
CHIP_BLOCKS = 4
WINDOW = CHIP_BLOCKS * (REACH_CHIPS + 1)
MAX_PAIRS = 5
QUARTER = BLK // N_KV
ROWS = HEADS_PER_GROUP * BLK
GROUP = HEADS_PER_GROUP * D
LOW_LOGIT = -1e30
INVERSE_ROOT = 1.0 / math.sqrt(D)
EXP2_FACTOR = INVERSE_ROOT / math.log(2.0)
F32 = jnp.float32
BF16 = jnp.bfloat16

NN = (((1,), (0,)), ((), ()))
NT = (((1,), (1,)), ((), ()))
TN = (((0,), (0,)), ((), ()))


def dot(a, b, dims=NN):
    return lax.dot_general(a, b, dims, preferred_element_type=F32)


def position(index):
    return N_KV * (index % QUARTER) + index // QUARTER


def attention_kernel(
    place_ref,
    parents_ref,
    q_ref,
    g_own_ref,
    g_other_ref,
    kv_here_ref,
    kv_one_ref,
    kv_two_ref,
    att_own_ref,
    att_other_ref,
    dq_ref,
    d_here_ref,
    d_one_ref,
    d_two_ref,
    tiles,
    keys,
    values,
    queries,
    grads,
    logits,
    peaks,
    attended,
    query_grad,
    weights,
    dlogits,
    key_grad,
    value_grad,
):
    chip = place_ref[0]
    core = place_ref[1]
    base = (chip - REACH_CHIPS) * CHIP_BLOCKS

    for source, ref in enumerate((kv_two_ref, kv_one_ref, kv_here_ref)):
        for block in range(CHIP_BLOCKS):
            window = source * CHIP_BLOCKS + block
            rows = slice((block % 2) * QUARTER, (block % 2 + 1) * QUARTER)
            for k in range(N_KV):
                out = slice(k * QUARTER, (k + 1) * QUARTER)
                keys[window, out, :] = ref[k, block // 2, rows, 0:D]
                values[window, out, :] = ref[k, block // 2, rows, D : 2 * D]
    key_grad[...] = jnp.zeros_like(key_grad)
    value_grad[...] = jnp.zeros_like(value_grad)

    row_i = lax.broadcasted_iota(jnp.int32, (BLK, BLK), 0)
    col_i = lax.broadcasted_iota(jnp.int32, (BLK, BLK), 1)
    to_slots = (position(row_i) == col_i).astype(BF16)
    to_tokens = (row_i == position(col_i)).astype(BF16)
    causal = position(row_i) >= position(col_i)

    def one_block(step, unused):
        slot = step // 2
        half = step % 2
        owner = jnp.where(slot == 0, core, 1 - core)
        own_window = REACH_CHIPS * CHIP_BLOCKS + owner * 2 + half
        quarter = pl.multiple_of(half * QUARTER, QUARTER)
        half_rows = pl.ds(pl.multiple_of(half * BLK, BLK), BLK)

        tiles[0] = own_window

        def climb(unused, running):
            current, count = running
            found = current >= 0

            @pl.when(found)
            def _():
                tiles[count + 2] = current - base

            following = parents_ref[jnp.maximum(current, 0)]
            return (
                jnp.where(found, following, -1),
                jnp.where(found, count + 1, count),
            )

        start = parents_ref[base + own_window]
        _, count = lax.fori_loop(0, 2 * MAX_PAIRS - 1, climb, (start, jnp.int32(0)))
        odd = count % 2 == 1
        tiles[1] = jnp.where(odd, tiles[jnp.where(odd, count + 1, 0)], own_window)
        pairs = count // 2 + 1

        for h in range(HEADS_PER_GROUP):
            for k in range(N_KV):
                queries[h * BLK + k * QUARTER : h * BLK + (k + 1) * QUARTER, :] = q_ref[
                    k, owner, pl.ds(quarter, QUARTER), h * D : (h + 1) * D
                ]

        def load_grads(ref):
            slots = dot(to_slots, ref[half_rows, :]).astype(BF16)
            for h in range(HEADS_PER_GROUP):
                grads[h * BLK : (h + 1) * BLK, :] = slots[:, h * D : (h + 1) * D]

        pl.when(slot == 0)(lambda: load_grads(g_own_ref))
        pl.when(slot == 1)(lambda: load_grads(g_other_ref))

        def pair_of(ref, pair):
            return jnp.concatenate([ref[tiles[2 * pair]], ref[tiles[2 * pair + 1]]], axis=0)

        first = dot(queries[...], pair_of(keys, 0), NT)
        for h in range(HEADS_PER_GROUP):
            rows = slice(h * BLK, (h + 1) * BLK)
            left = jnp.where(causal, first[rows, :BLK], LOW_LOGIT)
            right = jnp.where(odd, first[rows, BLK:], LOW_LOGIT)
            logits[0, rows, :BLK] = left
            logits[0, rows, BLK:] = right
            peaks[rows, :] = jnp.maximum(left, right)

        def logit_step(pair, unused):
            scores = dot(queries[...], pair_of(keys, pair), NT)
            logits[pair] = scores
            peaks[...] = jnp.maximum(
                peaks[...], jnp.maximum(scores[:, :BLK], scores[:, BLK:])
            )
            return unused

        lax.fori_loop(1, pairs, logit_step, 0)
        peak = jnp.max(peaks[...], axis=1, keepdims=True) * EXP2_FACTOR
        peaks[...] = jnp.broadcast_to(peak, (ROWS, BLK))
        attended[...] = jnp.zeros_like(attended)
        query_grad[...] = jnp.zeros_like(query_grad)

        def out_step(pair, unused):
            for h in range(HEADS_PER_GROUP):
                rows = slice(h * BLK, (h + 1) * BLK)
                peak = peaks[rows, :]
                left = jnp.exp2(logits[pair, rows, :BLK] * EXP2_FACTOR - peak)
                right = jnp.exp2(logits[pair, rows, BLK:] * EXP2_FACTOR - peak)
                logits[pair, rows, :BLK] = left
                logits[pair, rows, BLK:] = right
                weights[rows, :BLK] = left.astype(BF16)
                weights[rows, BLK:] = right.astype(BF16)
                query_grad[rows, :] += left + right
            attended[...] += dot(weights[...], pair_of(values, pair))
            return unused

        lax.fori_loop(0, pairs, out_step, 0)
        total = jnp.sum(query_grad[...], axis=1, keepdims=True)
        inverse = 1.0 / total
        rounded = (attended[...] * inverse).astype(BF16)
        row_dot = jnp.sum(
            grads[...].astype(F32) * rounded.astype(F32), axis=1, keepdims=True
        )
        peaks[...] = jnp.broadcast_to(inverse, (ROWS, BLK))
        attended[...] = jnp.broadcast_to(row_dot, (ROWS, BLK))
        wide = jnp.concatenate(
            [rounded[h * BLK : (h + 1) * BLK] for h in range(HEADS_PER_GROUP)], axis=1
        )
        in_tokens = dot(to_tokens, wide).astype(BF16)

        @pl.when(slot == 0)
        def _():
            att_own_ref[half_rows, :] = in_tokens

        @pl.when(slot == 1)
        def _():
            att_other_ref[half_rows, :] = in_tokens

        query_grad[...] = jnp.zeros_like(query_grad)

        def back_step(pair, unused):
            dprobs = dot(grads[...], pair_of(values, pair), NT)
            for h in range(HEADS_PER_GROUP):
                rows = slice(h * BLK, (h + 1) * BLK)
                for part in range(2):
                    cols = slice(part * BLK, (part + 1) * BLK)
                    probs = logits[pair, rows, cols] * peaks[rows, :]
                    weights[rows, cols] = probs.astype(BF16)
                    dlogits[rows, cols] = (
                        probs * (dprobs[rows, cols] - attended[rows, :])
                    ).astype(BF16)
            query_grad[...] += dot(dlogits[...], pair_of(keys, pair))
            key_part = dot(dlogits[...], queries[...], TN)
            value_part = dot(weights[...], grads[...], TN)
            for part in range(2):
                rows = slice(part * BLK, (part + 1) * BLK)
                window = tiles[2 * pair + part]
                key_grad[window] += key_part[rows, :]
                value_grad[window] += value_part[rows, :]
            return unused

        lax.fori_loop(0, pairs, back_step, 0)
        for h in range(HEADS_PER_GROUP):
            for k in range(N_KV):
                rows = slice(h * BLK + k * QUARTER, h * BLK + (k + 1) * QUARTER)
                dq_ref[k, owner, pl.ds(quarter, QUARTER), h * D : (h + 1) * D] = (
                    query_grad[rows, :] * INVERSE_ROOT
                ).astype(BF16)
        return unused

    lax.fori_loop(0, CHIP_BLOCKS, one_block, 0)

    for source, ref in enumerate((d_two_ref, d_one_ref, d_here_ref)):
        for block in range(CHIP_BLOCKS):
            window = source * CHIP_BLOCKS + block
            rows = slice((block % 2) * QUARTER, (block % 2 + 1) * QUARTER)
            for k in range(N_KV):
                part = slice(k * QUARTER, (k + 1) * QUARTER)
                ref[k, block // 2, rows, 0:D] = (
                    key_grad[window, part, :] * INVERSE_ROOT
                ).astype(ref.dtype)
                ref[k, block // 2, rows, D : 2 * D] = value_grad[window, part, :].astype(
                    ref.dtype
                )


def attention(place, parents, q, g_own, g_other, kv_here, kv_one, kv_two):
    vmem = pl.BlockSpec(memory_space=pltpu.VMEM)
    smem = pl.BlockSpec(memory_space=pltpu.SMEM)
    return pl.pallas_call(
        attention_kernel,
        out_shape=(
            jax.ShapeDtypeStruct(g_own.shape, BF16),
            pltpu.HBM(g_other.shape, BF16),
            jax.ShapeDtypeStruct(q.shape, BF16),
            pltpu.HBM(kv_here.shape, F32),
            pltpu.HBM(kv_one.shape, BF16),
            pltpu.HBM(kv_two.shape, BF16),
        ),
        in_specs=[smem, smem] + [vmem] * 6,
        out_specs=(pl.BlockSpec(),) * 6,
        scratch_shapes=[
            pltpu.SMEM((2 * MAX_PAIRS + 2,), jnp.int32),
            pltpu.VMEM((WINDOW, BLK, D), BF16),
            pltpu.VMEM((WINDOW, BLK, D), BF16),
            pltpu.VMEM((ROWS, D), BF16),
            pltpu.VMEM((ROWS, D), BF16),
            pltpu.VMEM((MAX_PAIRS, ROWS, 2 * BLK), F32),
            pltpu.VMEM((ROWS, BLK), F32),
            pltpu.VMEM((ROWS, D), F32),
            pltpu.VMEM((ROWS, D), F32),
            pltpu.VMEM((ROWS, 2 * BLK), BF16),
            pltpu.VMEM((ROWS, 2 * BLK), BF16),
            pltpu.VMEM((WINDOW, BLK, D), F32),
            pltpu.VMEM((WINDOW, BLK, D), F32),
        ],
        compiler_params=pltpu.CompilerParams(vmem_limit_bytes=48 << 20),
        name="tree_attention",
    )(place, parents, q, g_own, g_other, kv_here, kv_one, kv_two)


def pack_kernel(k_ref, v_ref, out_ref):
    for h in range(KEY_VALUE_HEADS):
        cols = slice(h * D, (h + 1) * D)
        out_ref[h, :, 0:D] = k_ref[:, cols]
        out_ref[h, :, D : 2 * D] = v_ref[:, cols]


def pack(k, v):
    rows = k.shape[0]
    return pl.pallas_call(
        pack_kernel,
        out_shape=jax.ShapeDtypeStruct((KEY_VALUE_HEADS, rows, 2 * D), k.dtype),
        name="pack_keys_values",
    )(k, v)


def unpack_kernel(in_ref, k_ref, v_ref):
    for h in range(KEY_VALUE_HEADS):
        cols = slice(h * D, (h + 1) * D)
        k_ref[:, cols] = in_ref[h, :, 0:D]
        v_ref[:, cols] = in_ref[h, :, D : 2 * D]


def unpack(value):
    rows = value.shape[1]
    flat = jax.ShapeDtypeStruct((rows, KEY_VALUE_HEADS * D), value.dtype)
    return pl.pallas_call(
        unpack_kernel, out_shape=(flat, flat), name="unpack_keys_values"
    )(value)


def add_kernel(here_ref, one_ref, two_ref, after_ref, out_ref):
    out_ref[...] = (
        here_ref[...] + one_ref[...].astype(F32) + two_ref[...].astype(F32)
    ).astype(BF16)


def add_parts(here, one, two, after):
    vmem = pl.BlockSpec(memory_space=pltpu.VMEM)
    return pl.pallas_call(
        add_kernel,
        out_shape=jax.ShapeDtypeStruct(here.shape, BF16),
        in_specs=[vmem, vmem, vmem, pl.BlockSpec(memory_space=pl.ANY)],
        out_specs=vmem,
        name="add_parts",
    )(here, one, two, after)


def along_chips(value, by):
    chips = lax.axis_size("chip")
    return lax.ppermute(value, "chip", [(i, (i + by) % chips) for i in range(chips)])


def core_swap(value):
    return lax.ppermute(value, "core", [(0, 1), (1, 0)])


def exchange(value):
    return lax.all_to_all(value, ("kv", "core"), split_axis=0, concat_axis=0, tiled=True)


def local(queries, key_state_rows, value_state_rows, output_gradient, parents):
    rows = queries.shape[0]
    core = lax.axis_index("core")
    chip = lax.axis_index("chip")
    groups = KEY_VALUE_HEADS

    kv_here = exchange(
        pack(
            key_state_rows.reshape(rows, groups * D),
            value_state_rows.reshape(rows, groups * D),
        )
    )
    q_send = queries.reshape(rows, groups, GROUP).transpose(1, 0, 2)
    g_own = lax.dynamic_slice_in_dim(output_gradient, core * GROUP, GROUP, axis=1)
    g_send = lax.dynamic_slice_in_dim(
        output_gradient, (1 - core) * GROUP, GROUP, axis=1
    )
    kv_here, q_send, g_own, g_send = lax.optimization_barrier(
        (kv_here, q_send, g_own, g_send)
    )
    kv_here = kv_here.reshape(N_KV, CORES, rows, 2 * D)
    g_other = core_swap(g_send)
    kv_one = along_chips(kv_here, 1)
    kv_two = along_chips(kv_here, 2)
    q = exchange(q_send).reshape(N_KV, CORES, rows, GROUP)
    place = jnp.stack([chip, core]).astype(jnp.int32)
    att_own, att_other, dq, d_here, d_one, d_two = attention(
        place, parents, q, g_own, g_other, kv_here, kv_one, kv_two
    )
    att_received = core_swap(att_other)
    attended = jnp.where(
        core == 0,
        jnp.concatenate([att_own, att_received], axis=1),
        jnp.concatenate([att_received, att_own], axis=1),
    )
    d_q = exchange(dq.reshape(groups, rows, GROUP))
    summed = add_parts(d_here, along_chips(d_one, -1), along_chips(d_two, -2), d_q)
    d_kv = exchange(summed.reshape(groups, rows, 2 * D)).transpose(1, 0, 2)
    d_k = d_kv[:, :, :D]
    d_v = d_kv[:, :, D:]
    return (
        attended,
        d_q.transpose(1, 0, 2).reshape(rows, 1, QUERY_HEADS * D),
        d_k.reshape(rows, 1, groups * D),
        d_v.reshape(rows, 1, groups * D),
    )


def solution(mesh):
    fine = Mesh(
        mesh.devices.reshape(mesh.shape["kv"], mesh.shape["seq"] // CORES, CORES),
        ("kv", "chip", "core"),
    )
    tokens = P(("chip", "core"), "kv", None)
    flat = P(("chip", "core"), "kv")
    return jax.shard_map(
        local,
        mesh=fine,
        in_specs=(tokens, tokens, tokens, flat, P()),
        out_specs=(flat, tokens, tokens, tokens),
        check_vma=False,
    )
```

```python
import functools
import math

import jax
import jax.numpy as jnp
from jax import lax
from jax.experimental import pallas as pl
from jax.experimental.pallas import tpu as pltpu
from jax.sharding import Mesh
from jax.sharding import PartitionSpec as P

QUERY_HEADS = 64
KEY_VALUE_HEADS = 8
HEADS_PER_GROUP = QUERY_HEADS // KEY_VALUE_HEADS
D = 128
BLK = 128
N_KV = 4
CORES = 2
REACH_CHIPS = 2
CHIP_BLOCKS = 4
WINDOW = CHIP_BLOCKS * (REACH_CHIPS + 1)
MAX_PAIRS = 5
QUARTER = BLK // N_KV
ROWS = HEADS_PER_GROUP * BLK
GROUP = HEADS_PER_GROUP * D
LOW_LOGIT = -1e30
INVERSE_ROOT = 1.0 / math.sqrt(D)
EXP2_FACTOR = INVERSE_ROOT / math.log(2.0)
F32 = jnp.float32
BF16 = jnp.bfloat16

NN = (((1,), (0,)), ((), ()))
NT = (((1,), (1,)), ((), ()))
TN = (((0,), (0,)), ((), ()))


def dot(a, b, dims=NN):
    return lax.dot_general(a, b, dims, preferred_element_type=F32)


def position(index):
    return N_KV * (index % QUARTER) + index // QUARTER


def attention_kernel(
    place_ref,
    parents_ref,
    q_ref,
    g_own_ref,
    g_other_ref,
    kv_here_ref,
    kv_one_ref,
    kv_two_ref,
    att_own_ref,
    att_other_ref,
    dq_ref,
    d_here_ref,
    d_one_ref,
    d_two_ref,
    tiles,
    keys,
    values,
    queries,
    grads,
    logits,
    peaks,
    attended,
    query_grad,
    weights,
    dlogits,
    key_grad,
    value_grad,
):
    chip = place_ref[0]
    core = place_ref[1]
    base = (chip - REACH_CHIPS) * CHIP_BLOCKS

    for source, ref in enumerate((kv_two_ref, kv_one_ref, kv_here_ref)):
        for block in range(CHIP_BLOCKS):
            window = source * CHIP_BLOCKS + block
            rows = slice((block % 2) * QUARTER, (block % 2 + 1) * QUARTER)
            for k in range(N_KV):
                out = slice(k * QUARTER, (k + 1) * QUARTER)
                keys[window, out, :] = ref[k, block // 2, rows, 0:D]
                values[window, out, :] = ref[k, block // 2, rows, D : 2 * D]
    key_grad[...] = jnp.zeros_like(key_grad)
    value_grad[...] = jnp.zeros_like(value_grad)

    row_i = lax.broadcasted_iota(jnp.int32, (BLK, BLK), 0)
    col_i = lax.broadcasted_iota(jnp.int32, (BLK, BLK), 1)
    to_slots = (position(row_i) == col_i).astype(BF16)
    to_tokens = (row_i == position(col_i)).astype(BF16)
    causal = position(row_i) >= position(col_i)

    def one_block(step, unused):
        slot = step // 2
        half = step % 2
        owner = jnp.where(slot == 0, core, 1 - core)
        own_window = REACH_CHIPS * CHIP_BLOCKS + owner * 2 + half
        quarter = pl.multiple_of(half * QUARTER, QUARTER)
        half_rows = pl.ds(pl.multiple_of(half * BLK, BLK), BLK)

        tiles[0] = own_window

        def climb(unused, running):
            current, count = running
            found = current >= 0

            @pl.when(found)
            def _():
                tiles[count + 2] = current - base

            following = parents_ref[jnp.maximum(current, 0)]
            return (
                jnp.where(found, following, -1),
                jnp.where(found, count + 1, count),
            )

        start = parents_ref[base + own_window]
        _, count = lax.fori_loop(0, 2 * MAX_PAIRS - 1, climb, (start, jnp.int32(0)))
        odd = count % 2 == 1
        tiles[1] = jnp.where(odd, tiles[jnp.where(odd, count + 1, 0)], own_window)
        pairs = count // 2 + 1

        for h in range(HEADS_PER_GROUP):
            for k in range(N_KV):
                queries[h * BLK + k * QUARTER : h * BLK + (k + 1) * QUARTER, :] = q_ref[
                    k, owner, pl.ds(quarter, QUARTER), h * D : (h + 1) * D
                ]

        def load_grads(ref):
            slots = dot(to_slots, ref[half_rows, :]).astype(BF16)
            for h in range(HEADS_PER_GROUP):
                grads[h * BLK : (h + 1) * BLK, :] = slots[:, h * D : (h + 1) * D]

        pl.when(slot == 0)(lambda: load_grads(g_own_ref))
        pl.when(slot == 1)(lambda: load_grads(g_other_ref))

        def pair_of(ref, pair):
            return jnp.concatenate([ref[tiles[2 * pair]], ref[tiles[2 * pair + 1]]], axis=0)

        first = dot(queries[...], pair_of(keys, 0), NT)
        for h in range(HEADS_PER_GROUP):
            rows = slice(h * BLK, (h + 1) * BLK)
            left = jnp.where(causal, first[rows, :BLK], LOW_LOGIT)
            right = jnp.where(odd, first[rows, BLK:], LOW_LOGIT)
            logits[0, rows, :BLK] = left
            logits[0, rows, BLK:] = right
            peaks[rows, :] = jnp.maximum(left, right)

        def logit_step(pair, unused):
            scores = dot(queries[...], pair_of(keys, pair), NT)
            logits[pair] = scores
            peaks[...] = jnp.maximum(
                peaks[...], jnp.maximum(scores[:, :BLK], scores[:, BLK:])
            )
            return unused

        lax.fori_loop(1, pairs, logit_step, 0)
        peak = jnp.max(peaks[...], axis=1, keepdims=True) * EXP2_FACTOR
        peaks[...] = jnp.broadcast_to(peak, (ROWS, BLK))
        attended[...] = jnp.zeros_like(attended)
        query_grad[...] = jnp.zeros_like(query_grad)

        def out_step(pair, unused):
            for h in range(HEADS_PER_GROUP):
                rows = slice(h * BLK, (h + 1) * BLK)
                peak = peaks[rows, :]
                left = jnp.exp2(logits[pair, rows, :BLK] * EXP2_FACTOR - peak)
                right = jnp.exp2(logits[pair, rows, BLK:] * EXP2_FACTOR - peak)
                logits[pair, rows, :BLK] = left
                logits[pair, rows, BLK:] = right
                weights[rows, :BLK] = left.astype(BF16)
                weights[rows, BLK:] = right.astype(BF16)
                query_grad[rows, :] += left + right
            attended[...] += dot(weights[...], pair_of(values, pair))
            return unused

        lax.fori_loop(0, pairs, out_step, 0)
        total = jnp.sum(query_grad[...], axis=1, keepdims=True)
        inverse = 1.0 / total
        rounded = (attended[...] * inverse).astype(BF16)
        row_dot = jnp.sum(
            grads[...].astype(F32) * rounded.astype(F32), axis=1, keepdims=True
        )
        peaks[...] = jnp.broadcast_to(inverse, (ROWS, BLK))
        attended[...] = jnp.broadcast_to(row_dot, (ROWS, BLK))
        wide = jnp.concatenate(
            [rounded[h * BLK : (h + 1) * BLK] for h in range(HEADS_PER_GROUP)], axis=1
        )
        in_tokens = dot(to_tokens, wide).astype(BF16)

        @pl.when(slot == 0)
        def _():
            att_own_ref[half_rows, :] = in_tokens

        @pl.when(slot == 1)
        def _():
            att_other_ref[half_rows, :] = in_tokens

        query_grad[...] = jnp.zeros_like(query_grad)

        def back_step(pair, unused):
            dprobs = dot(grads[...], pair_of(values, pair), NT)
            for h in range(HEADS_PER_GROUP):
                rows = slice(h * BLK, (h + 1) * BLK)
                for part in range(2):
                    cols = slice(part * BLK, (part + 1) * BLK)
                    probs = logits[pair, rows, cols] * peaks[rows, :]
                    weights[rows, cols] = probs.astype(BF16)
                    dlogits[rows, cols] = (
                        probs * (dprobs[rows, cols] - attended[rows, :])
                    ).astype(BF16)
            query_grad[...] += dot(dlogits[...], pair_of(keys, pair))
            key_part = dot(dlogits[...], queries[...], TN)
            value_part = dot(weights[...], grads[...], TN)
            for part in range(2):
                rows = slice(part * BLK, (part + 1) * BLK)
                window = tiles[2 * pair + part]
                key_grad[window] += key_part[rows, :]
                value_grad[window] += value_part[rows, :]
            return unused

        lax.fori_loop(0, pairs, back_step, 0)
        for h in range(HEADS_PER_GROUP):
            for k in range(N_KV):
                rows = slice(h * BLK + k * QUARTER, h * BLK + (k + 1) * QUARTER)
                dq_ref[k, owner, pl.ds(quarter, QUARTER), h * D : (h + 1) * D] = (
                    query_grad[rows, :] * INVERSE_ROOT
                ).astype(BF16)
        return unused

    lax.fori_loop(0, CHIP_BLOCKS, one_block, 0)

    for source, ref in enumerate((d_two_ref, d_one_ref, d_here_ref)):
        for block in range(CHIP_BLOCKS):
            window = source * CHIP_BLOCKS + block
            rows = slice((block % 2) * QUARTER, (block % 2 + 1) * QUARTER)
            for k in range(N_KV):
                part = slice(k * QUARTER, (k + 1) * QUARTER)
                ref[k, block // 2, rows, 0:D] = (
                    key_grad[window, part, :] * INVERSE_ROOT
                ).astype(ref.dtype)
                ref[k, block // 2, rows, D : 2 * D] = value_grad[window, part, :].astype(
                    ref.dtype
                )


def attention(place, parents, q, g_own, g_other, kv_here, kv_one, kv_two):
    vmem = pl.BlockSpec(memory_space=pltpu.VMEM)
    smem = pl.BlockSpec(memory_space=pltpu.SMEM)
    return pl.pallas_call(
        attention_kernel,
        out_shape=(
            jax.ShapeDtypeStruct(g_own.shape, BF16),
            pltpu.HBM(g_other.shape, BF16),
            jax.ShapeDtypeStruct(q.shape, BF16),
            pltpu.HBM(kv_here.shape, F32),
            pltpu.HBM(kv_one.shape, BF16),
            pltpu.HBM(kv_two.shape, BF16),
        ),
        in_specs=[smem, smem] + [vmem] * 6,
        out_specs=(pl.BlockSpec(),) * 6,
        scratch_shapes=[
            pltpu.SMEM((2 * MAX_PAIRS + 2,), jnp.int32),
            pltpu.VMEM((WINDOW, BLK, D), BF16),
            pltpu.VMEM((WINDOW, BLK, D), BF16),
            pltpu.VMEM((ROWS, D), BF16),
            pltpu.VMEM((ROWS, D), BF16),
            pltpu.VMEM((MAX_PAIRS, ROWS, 2 * BLK), F32),
            pltpu.VMEM((ROWS, BLK), F32),
            pltpu.VMEM((ROWS, D), F32),
            pltpu.VMEM((ROWS, D), F32),
            pltpu.VMEM((ROWS, 2 * BLK), BF16),
            pltpu.VMEM((ROWS, 2 * BLK), BF16),
            pltpu.VMEM((WINDOW, BLK, D), F32),
            pltpu.VMEM((WINDOW, BLK, D), F32),
        ],
        compiler_params=pltpu.CompilerParams(vmem_limit_bytes=48 << 20),
        name="tree_attention",
    )(place, parents, q, g_own, g_other, kv_here, kv_one, kv_two)


def pack_kernel(k_ref, v_ref, out_ref):
    for h in range(KEY_VALUE_HEADS):
        cols = slice(h * D, (h + 1) * D)
        out_ref[h, :, 0:D] = k_ref[:, cols]
        out_ref[h, :, D : 2 * D] = v_ref[:, cols]


def pack(k, v):
    rows = k.shape[0]
    return pl.pallas_call(
        pack_kernel,
        out_shape=jax.ShapeDtypeStruct((KEY_VALUE_HEADS, rows, 2 * D), k.dtype),
        name="pack_keys_values",
    )(k, v)


def unpack_kernel(in_ref, k_ref, v_ref):
    for h in range(KEY_VALUE_HEADS):
        cols = slice(h * D, (h + 1) * D)
        k_ref[:, cols] = in_ref[h, :, 0:D]
        v_ref[:, cols] = in_ref[h, :, D : 2 * D]


def unpack(value):
    rows = value.shape[1]
    flat = jax.ShapeDtypeStruct((rows, KEY_VALUE_HEADS * D), value.dtype)
    return pl.pallas_call(
        unpack_kernel, out_shape=(flat, flat), name="unpack_keys_values"
    )(value)


def add_kernel(here_ref, one_ref, two_ref, after_ref, out_ref):
    out_ref[...] = (
        here_ref[...] + one_ref[...].astype(F32) + two_ref[...].astype(F32)
    ).astype(BF16)


def add_parts(here, one, two, after):
    vmem = pl.BlockSpec(memory_space=pltpu.VMEM)
    return pl.pallas_call(
        add_kernel,
        out_shape=jax.ShapeDtypeStruct(here.shape, BF16),
        in_specs=[vmem, vmem, vmem, pl.BlockSpec(memory_space=pl.ANY)],
        out_specs=vmem,
        name="add_parts",
    )(here, one, two, after)


def along_chips(value, by):
    chips = lax.axis_size("chip")
    return lax.ppermute(value, "chip", [(i, (i + by) % chips) for i in range(chips)])


def core_swap(value):
    return lax.ppermute(value, "core", [(0, 1), (1, 0)])


def exchange(value):
    return lax.all_to_all(value, ("kv", "core"), split_axis=0, concat_axis=0, tiled=True)


def local(queries, key_state_rows, value_state_rows, output_gradient, parents):
    rows = queries.shape[0]
    core = lax.axis_index("core")
    chip = lax.axis_index("chip")
    groups = KEY_VALUE_HEADS

    kv_here = exchange(
        pack(
            key_state_rows.reshape(rows, groups * D),
            value_state_rows.reshape(rows, groups * D),
        )
    )
    q_send = queries.reshape(rows, groups, GROUP).transpose(1, 0, 2)
    g_own = lax.dynamic_slice_in_dim(output_gradient, core * GROUP, GROUP, axis=1)
    g_send = lax.dynamic_slice_in_dim(
        output_gradient, (1 - core) * GROUP, GROUP, axis=1
    )
    kv_here, q_send, g_own, g_send = lax.optimization_barrier(
        (kv_here, q_send, g_own, g_send)
    )
    kv_here = kv_here.reshape(N_KV, CORES, rows, 2 * D)
    g_other = core_swap(g_send)
    kv_one = along_chips(kv_here, 1)
    kv_two = along_chips(kv_here, 2)
    q = exchange(q_send).reshape(N_KV, CORES, rows, GROUP)
    place = jnp.stack([chip, core]).astype(jnp.int32)
    att_own, att_other, dq, d_here, d_one, d_two = attention(
        place, parents, q, g_own, g_other, kv_here, kv_one, kv_two
    )
    att_received = core_swap(att_other)
    attended = jnp.where(
        core == 0,
        jnp.concatenate([att_own, att_received], axis=1),
        jnp.concatenate([att_received, att_own], axis=1),
    )
    summed = (
        d_here
        + along_chips(d_one, -1).astype(F32)
        + along_chips(d_two, -2).astype(F32)
    ).astype(BF16)
    d_q, summed = lax.optimization_barrier(
        (exchange(dq.reshape(groups, rows, GROUP)), summed)
    )
    d_kv = exchange(summed.reshape(groups, rows, 2 * D)).transpose(1, 0, 2)
    d_k = d_kv[:, :, :D]
    d_v = d_kv[:, :, D:]
    return (
        attended,
        d_q.transpose(1, 0, 2).reshape(rows, 1, QUERY_HEADS * D),
        d_k.reshape(rows, 1, groups * D),
        d_v.reshape(rows, 1, groups * D),
    )


def solution(mesh):
    fine = Mesh(
        mesh.devices.reshape(mesh.shape["kv"], mesh.shape["seq"] // CORES, CORES),
        ("kv", "chip", "core"),
    )
    tokens = P(("chip", "core"), "kv", None)
    flat = P(("chip", "core"), "kv")
    return jax.shard_map(
        local,
        mesh=fine,
        in_specs=(tokens, tokens, tokens, flat, P()),
        out_specs=(flat, tokens, tokens, tokens),
        check_vma=False,
    )
```
